32 devices in a mesh: dp: 16 (over z, y, core), tensor: 2 (over x).
Axes of the slice: x: 2, y: 2, z: 4, core: 2. Of those that a mesh axis runs over, the one named last changes fastest.
Arguments:
- tokens: bfloat16 [4096, 768], P('dp'), may hold values from -6 to 6
- cotangent: bfloat16 [4096, 768], P('dp'), may hold values from -6 to 6
- segment: int32 [4096], P('dp'), may hold values from 0 to 15, as said below
- first_gain: float32 [768], replicated, may hold values from 0.1 to 1.9
- first_shift: float32 [768], replicated, may hold values from -1.75 to 1.75
- second_gain: float32 [768], replicated, may hold values from 0.1 to 1.9
- second_shift: float32 [768], replicated, may hold values from -1.75 to 1.75
- attend_weight: bfloat16 [768, 3, 768], P(None, None, 'tensor'), may hold values from -0.21875 to 0.21875
- attend_bias: float32 [3, 768], P(None, 'tensor'), may hold values from -13 to 13
- output_weight: bfloat16 [768, 768], P('tensor'), may hold values from -0.875 to 0.875
- output_bias: float32 [768], replicated, may hold values from -1.75 to 1.75
- expand_weight: bfloat16 [768, 3072], P(None, 'tensor'), may hold values from -0.21875 to 0.21875
- expand_bias: float32 [3072], P('tensor'), may hold values from -3 to 3
- shrink_weight: bfloat16 [3072, 768], P('tensor'), may hold values from -0.109375 to 0.109375
- shrink_bias: float32 [768], replicated, may hold values from -1.75 to 1.75
Outputs:
- result: bfloat16 [4096, 768], P('dp')
- input_grad: bfloat16 [4096, 768], P('dp')
- first_gain_grad: float32 [768], P('dp')
- first_shift_grad: float32 [768], P('dp')
- second_gain_grad: float32 [768], P('dp')
- second_shift_grad: float32 [768], P('dp')
- attend_weight_grad: float32 [768, 3, 768], P('dp', None, 'tensor')
- attend_bias_grad: float32 [3, 768], P(None, ('tensor', 'dp'))
- output_weight_grad: float32 [768, 768], P('tensor', 'dp')
- output_bias_grad: float32 [768], P('dp')
- expand_weight_grad: float32 [768, 3072], P('dp', 'tensor')
- expand_bias_grad: float32 [3072], P(('tensor', 'dp'))
- shrink_weight_grad: float32 [3072, 768], P('tensor', 'dp')
- shrink_bias_grad: float32 [768], P('dp')
The draws below stay inside these ranges and needn't reach their ends.
Inputs may be any that keep to these rules, and one draw needn't show every extreme that they name: Within the 256 tokens of each index of dp, segment numbers start at 0, never fall and rise by at most one from one token to the next; a document never spans two indices of dp; a block holds at most 16 documents, and some block holds that many.
All inputs are finite; a program needn't handle non-finite values.
Results may differ from the reference program's by a relative error of at most 0.012.
The reference program's roundings to bfloat16 on the way (of `mixed`, `active`, `lower_hidden`, `grad_mixed`, `grad_scores` and `lower_projected`) count: a program that leaves them out, or rounds other values in their place, can miss the bound.
Values may be sent and summed in bfloat16 or wider, within the bound.
A program may use at most 128 MiB of HBM per device.

```python
import jax
import jax.numpy as jnp
from jax import lax

D = 768
HEAD_DIM = 64
ROT = 16
FF = 3072
CAP = 256
TOKENS = 4096


def draw_segment(key, part):
    blocks = TOKENS // CAP
    most_docs = CAP // 16
    spacing = CAP // most_docs
    rate_key = jax.random.fold_in(key, 11)
    start_key = jax.random.fold_in(key, 12)
    rates = jax.random.randint(rate_key, (blocks, 1), 2, 64)
    throws = jax.random.randint(start_key, (blocks, CAP), 0, 1024)
    place = jnp.arange(CAP, dtype=jnp.int32)[None, :]
    leading = place == 0
    first_block = jnp.arange(blocks, dtype=jnp.int32)[:, None] == 0
    forced = jnp.logical_and(first_block, place % spacing == 0)
    starts = jnp.logical_or(jnp.logical_or(throws < rates, leading), forced).astype(jnp.int32)
    numbers = jnp.minimum(jnp.cumsum(starts, axis=1) - 1, most_docs - 1)
    return numbers.astype(jnp.int32).reshape(TOKENS)


def draw_attend_bias(key, part):
    noise = jax.random.normal(jax.random.fold_in(key, 21), (3, D), jnp.float32)
    base = 0.3 * jnp.clip(noise, -6.0, 6.0)
    return base


def block_scale(stream_key, dims, shards, low, top_value):
    level = 1.0
    for dim, parts in shards:
        draws = jax.random.uniform(jax.random.fold_in(jax.random.fold_in(stream_key, 6), dim), (parts,), jnp.float32, low / len(shards), top_value / len(shards))
        level = level * jnp.repeat(jnp.exp(draws), dims[dim] // parts).reshape((-1,) + (1,) * (len(dims) - 1 - dim))
    return level


def scatter_about(key, shape, scale, most, cuts=(), kind=jnp.bfloat16):
    array = jax.random.normal(key, shape, jnp.float32) * scale
    if len(cuts) > 0:
        array = block_scale(key, shape, cuts, -0.22, 0.18) * array
    return jnp.clip(array, min=-most, max=most).astype(kind)


def setup_inputs(seed: int = 0) -> dict:
    splits = jax.random.split(jax.random.key(seed), 16)
    tokens = scatter_about(splits[0], (TOKENS, D), 1.0, 6.0, ((0, 16),))
    cotangent = scatter_about(splits[1], (TOKENS, D), 1.0, 6.0, ((0, 16),))
    segment = draw_segment(jax.random.fold_in(splits[15], 71), 0)
    first_gain = jnp.clip(1.0 + 0.18 * jax.random.normal(splits[3], (D,), jnp.float32), 0.1, 1.9)
    first_shift = scatter_about(splits[4], (D,), 0.3, 1.75, (), jnp.float32)
    second_gain = jnp.clip(1.0 + 0.18 * jax.random.normal(splits[5], (D,), jnp.float32), 0.1, 1.9)
    second_shift = scatter_about(splits[6], (D,), 0.3, 1.75, (), jnp.float32)
    attend_weight = scatter_about(splits[7], (D, 3, D), D ** -0.5, 0.21875, ((2, 2),))
    attend_bias = draw_attend_bias(jax.random.fold_in(splits[15], 71), 0)
    output_weight = scatter_about(splits[9], (D, D), (D // 16) ** -0.5, 0.875, ((0, 2),))
    output_bias = scatter_about(splits[10], (D,), 0.3, 1.75, (), jnp.float32)
    expand_weight = scatter_about(splits[11], (D, FF), D ** -0.5, 0.21875, ((1, 2),))
    expand_bias = scatter_about(splits[12], (FF,), 0.5, 3.0, ((0, 2),), jnp.float32)
    shrink_weight = scatter_about(splits[13], (FF, D), FF ** -0.5, 0.109375, ((0, 2),))
    shrink_bias = scatter_about(splits[14], (D,), 0.3, 1.75, (), jnp.float32)
    return {"tokens": tokens, "cotangent": cotangent, "segment": segment, "first_gain": first_gain, "first_shift": first_shift, "second_gain": second_gain, "second_shift": second_shift, "attend_weight": attend_weight, "attend_bias": attend_bias, "output_weight": output_weight, "output_bias": output_bias, "expand_weight": expand_weight, "expand_bias": expand_bias, "shrink_weight": shrink_weight, "shrink_bias": shrink_bias}


EPSILON = 1e-05

def layer_norm(values, gain, shift):
    center = values - lax.optimization_barrier(jnp.mean(values, axis=-1, keepdims=True))
    spread = lax.optimization_barrier(jnp.mean(center * center, axis=-1, keepdims=True))
    inverse = lax.rsqrt(spread + EPSILON)
    scaled = center * inverse
    return (scaled, inverse, scaled * gain + shift)

def norm_back(grad_out, scaled, inverse, gain):
    grad_scaled = grad_out * gain
    first = lax.optimization_barrier(jnp.mean(grad_scaled, axis=-1, keepdims=True))
    second = lax.optimization_barrier(jnp.mean(grad_scaled * scaled, axis=-1, keepdims=True))
    return inverse * (grad_scaled - first - scaled * second)

def positions(segment):
    earlier = (segment[None, :] < segment[:, None]).astype(jnp.int32)
    starts = lax.optimization_barrier(jnp.sum(earlier, axis=1)).astype(jnp.int32)
    return (jnp.arange(segment.shape[0], dtype=jnp.int32) - starts).astype(jnp.float32)

def rotary_tables(places):
    half = ROT // 2
    freqs = 10000.0 ** (-(2.0 * jnp.arange(half, dtype=jnp.float32)) / ROT)
    angle = places[:, None] * freqs[None, :]
    cosine = jnp.concatenate([jnp.cos(angle), jnp.cos(angle)], axis=-1)[:, None, :]
    sine = jnp.concatenate([jnp.sin(angle), jnp.sin(angle)], axis=-1)[:, None, :]
    return (cosine, sine)

def rotate(values, cosine, sine):
    half = ROT // 2
    part = values[..., :ROT]
    turned = jnp.concatenate([-part[..., half:], part[..., :half]], axis=-1)
    return jnp.concatenate([part * cosine + turned * sine, values[..., ROT:]], axis=-1)

def unrotate(grads, cosine, sine):
    half = ROT // 2
    part = grads[..., :ROT]
    weighted = part * sine
    back = jnp.concatenate([weighted[..., half:], -weighted[..., :half]], axis=-1)
    return jnp.concatenate([part * cosine + back, grads[..., ROT:]], axis=-1)

def gelu_slope(values):
    normal_cdf = 0.5 * (1.0 + lax.erf(values * 0.7071067811865476))
    density = jnp.exp(-0.5 * values * values) * 0.3989422804014327
    return normal_cdf + values * density

def attend_mask(segment):
    index = jnp.arange(segment.shape[0], dtype=jnp.int32)
    return jnp.logical_and(segment[:, None] == segment[None, :], index[None, :] <= index[:, None])

def product(form, left, right):
    return jnp.einsum(form, left.astype(jnp.float32), right.astype(jnp.float32))

def scores_of(queries, keys_rot, allowed):
    raw = product('ihd,jhd->hij', queries, keys_rot) * HEAD_DIM ** (-0.5)
    return jnp.where(allowed[None], raw, -1e+30)

def one_block(params, pieces):
    first_gain, first_shift, second_gain, second_shift, attend_weight, attend_bias, output_weight, output_bias, expand_weight, expand_bias, shrink_weight, shrink_bias = params
    tokens, cotangent, segment = pieces
    count = tokens.shape[0]
    heads_here = attend_weight.shape[2] // HEAD_DIM
    stream = tokens.astype(jnp.float32)
    cosine, sine = rotary_tables(positions(segment))
    allowed = attend_mask(segment)
    scaled_one, inverse_one, normed_one = layer_norm(stream, first_gain, first_shift)
    scaled_two, inverse_two, normed_two = layer_norm(stream, second_gain, second_shift)
    lower_one = normed_one.astype(jnp.bfloat16)
    lower_two = normed_two.astype(jnp.bfloat16)
    projected = product('cd,dtf->ctf', lower_one, attend_weight) + attend_bias
    queries = rotate(projected[:, 0].reshape(count, heads_here, HEAD_DIM), cosine, sine).astype(jnp.bfloat16)
    keys_rot = rotate(projected[:, 1].reshape(count, heads_here, HEAD_DIM), cosine, sine).astype(jnp.bfloat16)
    values = projected[:, 2].reshape(count, heads_here, HEAD_DIM).astype(jnp.bfloat16)
    scores = scores_of(queries, keys_rot, allowed)
    top = lax.optimization_barrier(jnp.max(scores, axis=2, keepdims=True))
    expsum = jnp.where(allowed[None], jnp.exp(scores - top), 0.0)
    total = lax.optimization_barrier(jnp.sum(expsum, axis=2, keepdims=True))
    logsum = top + jnp.log(total)
    probs = (expsum / total).astype(jnp.bfloat16)
    mixed = product('hij,jhd->ihd', probs, values).reshape(count, -1).astype(jnp.bfloat16)
    hidden = jnp.dot(lower_two, expand_weight, preferred_element_type=jnp.float32) + expand_bias
    active = jax.nn.gelu(hidden, approximate=False).astype(jnp.bfloat16)
    branches = jnp.dot(mixed, output_weight, preferred_element_type=jnp.float32)
    branches = branches + jnp.dot(active, shrink_weight, preferred_element_type=jnp.float32)
    result = (stream + branches + output_bias + shrink_bias).astype(jnp.bfloat16)
    upstream = cotangent.astype(jnp.float32)
    column_sum = lax.optimization_barrier(jnp.sum(upstream, axis=0))
    grad_shrink = jnp.dot(active.T, cotangent, preferred_element_type=jnp.float32)
    grad_active = jnp.dot(cotangent, shrink_weight.T, preferred_element_type=jnp.float32)
    grad_hidden = grad_active * gelu_slope(hidden)
    expand_bias_grad = lax.optimization_barrier(jnp.sum(grad_hidden, axis=0))
    lower_hidden = grad_hidden.astype(jnp.bfloat16)
    grad_expand = jnp.dot(lower_two.T, lower_hidden, preferred_element_type=jnp.float32)
    grad_norm_two = jnp.dot(lower_hidden, expand_weight.T, preferred_element_type=jnp.float32)
    grad_output = jnp.dot(mixed.T, cotangent, preferred_element_type=jnp.float32)
    grad_mixed = jnp.dot(cotangent, output_weight.T, preferred_element_type=jnp.float32)
    grad_mixed = grad_mixed.astype(jnp.bfloat16).reshape(count, heads_here, HEAD_DIM)
    again = scores_of(queries, keys_rot, allowed)
    again_probs = jnp.where(allowed[None], jnp.exp(again - logsum), 0.0)
    grad_probs = product('ihd,jhd->hij', grad_mixed, values)
    grad_values = product('hij,ihd->jhd', again_probs.astype(jnp.bfloat16), grad_mixed)
    inner = lax.optimization_barrier(jnp.sum(again_probs * grad_probs, axis=2, keepdims=True))
    grad_scores = (again_probs * (grad_probs - inner) * HEAD_DIM ** (-0.5)).astype(jnp.bfloat16)
    grad_queries = unrotate(product('hij,jhd->ihd', grad_scores, keys_rot), cosine, sine)
    grad_keys = unrotate(product('hij,ihd->jhd', grad_scores, queries), cosine, sine)
    grad_projected = jnp.stack([grad_queries.reshape(count, -1), grad_keys.reshape(count, -1), grad_values.reshape(count, -1)], axis=1)
    attend_bias_grad = lax.optimization_barrier(jnp.sum(grad_projected, axis=0))
    lower_projected = grad_projected.astype(jnp.bfloat16)
    grad_attend = product('cd,ctf->dtf', lower_one, lower_projected)
    grad_norm_one = product('ctf,dtf->cd', lower_projected, attend_weight)
    grad_input = upstream + norm_back(grad_norm_one, scaled_one, inverse_one, first_gain)
    grad_input = grad_input + norm_back(grad_norm_two, scaled_two, inverse_two, second_gain)
    grads = (lax.optimization_barrier(jnp.sum(grad_norm_one * scaled_one, axis=0)), lax.optimization_barrier(jnp.sum(grad_norm_one, axis=0)), lax.optimization_barrier(jnp.sum(grad_norm_two * scaled_two, axis=0)), lax.optimization_barrier(jnp.sum(grad_norm_two, axis=0)), grad_attend, attend_bias_grad, grad_output, column_sum, grad_expand, expand_bias_grad, grad_shrink)
    return (result, grad_input.astype(jnp.bfloat16), grads)

def reference(tokens, cotangent, segment, first_gain, first_shift, second_gain, second_shift, attend_weight, attend_bias, output_weight, output_bias, expand_weight, expand_bias, shrink_weight, shrink_bias):
    blocks = TOKENS // CAP
    params = (first_gain, first_shift, second_gain, second_shift, attend_weight, attend_bias, output_weight, output_bias, expand_weight, expand_bias, shrink_weight, shrink_bias)
    pieces = (tokens.reshape(blocks, CAP, D), cotangent.reshape(blocks, CAP, D), segment.reshape(blocks, CAP).astype(jnp.int32))
    zeros = (jnp.zeros((D,), jnp.float32), jnp.zeros((D,), jnp.float32), jnp.zeros((D,), jnp.float32), jnp.zeros((D,), jnp.float32), jnp.zeros((D, 3, D), jnp.float32), jnp.zeros((3, D), jnp.float32), jnp.zeros((D, D), jnp.float32), jnp.zeros((D,), jnp.float32), jnp.zeros((D, FF), jnp.float32), jnp.zeros((FF,), jnp.float32), jnp.zeros((FF, D), jnp.float32))

    def step(carry, piece):
        result, grad_input, grads = one_block(params, piece)
        return (tuple((left + right for left, right in zip(carry, grads))), (result, grad_input))
    sums, outputs = lax.scan(step, zeros, pieces)
    return (outputs[0].reshape(TOKENS, D), outputs[1].reshape(TOKENS, D), sums[0], sums[1], sums[2], sums[3], sums[4], sums[5], sums[6], sums[7], sums[8], sums[9], sums[10], sums[7])
```

```python
import jax
import jax.numpy as jnp
from jax import lax
from jax.sharding import PartitionSpec as P

HEAD_DIM = 64
ROT = 16


EPSILON = 1e-05


def exchange_sum(part, axis):
    size = lax.axis_size(axis)
    part = part.astype(jnp.bfloat16)
    if size != 2:
        return lax.psum(part.astype(jnp.float32), axis)
    other = lax.ppermute(part, axis, [(0, 1), (1, 0)])
    return part.astype(jnp.float32) + other.astype(jnp.float32)


def block_order(bits, size):
    table = []
    for place in range(size):
        relative = 0
        for stage, bit in enumerate(bits):
            if (place >> (len(bits) - 1 - stage)) & 1:
                relative |= 1 << bit
        table.append(relative)
    return table


def picker(bits, size, width):
    block = width // size
    table = jnp.array(block_order(bits, size), dtype=jnp.int32)
    owner = jnp.bitwise_xor(table, lax.axis_index("dp").astype(jnp.int32))
    source = (owner[:, None] * block + jnp.arange(block, dtype=jnp.int32)[None, :]).reshape(-1)
    return (jnp.arange(width, dtype=jnp.int32)[:, None] == source[None, :]).astype(jnp.bfloat16)


def swap(value, bit):
    size = lax.axis_size("dp")
    return lax.ppermute(value, "dp", [(i, i ^ (1 << bit)) for i in range(size)])


def halve(kept, arrived, bits):
    total = kept + arrived
    for bit in bits:
        half = total.shape[0] // 2
        total = total[:half] + swap(total[half:], bit)
    return total


def weight_sum(rows, columns, bits):
    half = rows.shape[1] // 2

    def product(part):
        return jnp.einsum("cd,cf->df", part, columns, preferred_element_type=jnp.float32)

    arrived = swap(product(rows[:, half:]), bits[0])
    return halve(product(rows[:, :half]), arrived, bits[1:])


def layer_norm(values, gain, shift):
    center = values - jnp.mean(values, axis=-1, keepdims=True)
    spread = jnp.mean(center * center, axis=-1, keepdims=True)
    inverse = lax.rsqrt(spread + EPSILON)
    scaled = center * inverse
    return (scaled, inverse, scaled * gain + shift)


def norm_back(grad_out, scaled, inverse, gain):
    grad_scaled = grad_out * gain
    first = jnp.mean(grad_scaled, axis=-1, keepdims=True)
    second = jnp.mean(grad_scaled * scaled, axis=-1, keepdims=True)
    return inverse * (grad_scaled - first - scaled * second)


def positions(segment):
    earlier = (segment[None, :] < segment[:, None]).astype(jnp.int32)
    starts = jnp.sum(earlier, axis=1)
    return (jnp.arange(segment.shape[0], dtype=jnp.int32) - starts).astype(jnp.float32)


def rotary_tables(places):
    half = ROT // 2
    freqs = 10000.0 ** (-(2.0 * jnp.arange(half, dtype=jnp.float32)) / ROT)
    angle = places[:, None] * freqs[None, :]
    cosine = jnp.concatenate([jnp.cos(angle), jnp.cos(angle)], axis=-1)[:, None, :]
    sine = jnp.concatenate([jnp.sin(angle), jnp.sin(angle)], axis=-1)[:, None, :]
    return (cosine, sine)


def rotate(values, cosine, sine):
    half = ROT // 2
    part = values[..., :ROT]
    turned = jnp.concatenate([-part[..., half:], part[..., :half]], axis=-1)
    return jnp.concatenate([part * cosine + turned * sine, values[..., ROT:]], axis=-1)


def unrotate(grads, cosine, sine):
    half = ROT // 2
    part = grads[..., :ROT]
    weighted = part * sine
    back = jnp.concatenate([weighted[..., half:], -weighted[..., :half]], axis=-1)
    return jnp.concatenate([part * cosine + back, grads[..., ROT:]], axis=-1)


def gelu_slope(values):
    normal_cdf = 0.5 * (1.0 + lax.erf(values * 0.7071067811865476))
    density = jnp.exp(-0.5 * values * values) * 0.3989422804014327
    return normal_cdf + values * density


def attend_mask(segment):
    index = jnp.arange(segment.shape[0], dtype=jnp.int32)
    return jnp.logical_and(segment[:, None] == segment[None, :], index[None, :] <= index[:, None])


def scores_of(queries, keys_rot, allowed):
    raw = jnp.einsum("ihd,jhd->hij", queries, keys_rot, preferred_element_type=jnp.float32)
    return jnp.where(allowed[None], raw * HEAD_DIM ** (-0.5), -1e30)


def local(
    tokens,
    cotangent,
    segment,
    first_gain,
    first_shift,
    second_gain,
    second_shift,
    attend_weight,
    attend_bias,
    output_weight,
    output_bias,
    expand_weight,
    expand_bias,
    shrink_weight,
    shrink_bias,
):
    count = tokens.shape[0]
    heads_here = attend_weight.shape[2] // HEAD_DIM
    size = lax.axis_size("dp")
    near_first = list(range(size.bit_length() - 1))
    far_first = near_first[:1] + near_first[2:] + near_first[1:2]
    stream = tokens.astype(jnp.float32)
    cosine, sine = rotary_tables(positions(segment))
    allowed = attend_mask(segment)
    scaled_one, inverse_one, normed_one = layer_norm(stream, first_gain, first_shift)
    scaled_two, inverse_two, normed_two = layer_norm(stream, second_gain, second_shift)
    lower_one = normed_one.astype(jnp.bfloat16)
    lower_two = normed_two.astype(jnp.bfloat16)
    projected = (
        jnp.einsum("cd,dtf->ctf", lower_one, attend_weight, preferred_element_type=jnp.float32)
        + attend_bias
    )
    queries = rotate(projected[:, 0].reshape(count, heads_here, HEAD_DIM), cosine, sine).astype(
        jnp.bfloat16
    )
    keys_rot = rotate(projected[:, 1].reshape(count, heads_here, HEAD_DIM), cosine, sine).astype(
        jnp.bfloat16
    )
    values = projected[:, 2].reshape(count, heads_here, HEAD_DIM).astype(jnp.bfloat16)
    scores = scores_of(queries, keys_rot, allowed)
    top = jnp.max(scores, axis=2, keepdims=True)
    expsum = jnp.where(allowed[None], jnp.exp(scores - top), 0.0)
    total = jnp.sum(expsum, axis=2, keepdims=True)
    logsum = top + jnp.log(total)
    probs = (expsum / total).astype(jnp.bfloat16)
    mixed = jnp.einsum("hij,jhd->ihd", probs, values, preferred_element_type=jnp.float32)
    mixed = mixed.reshape(count, -1).astype(jnp.bfloat16)
    hidden = jnp.dot(lower_two, expand_weight, preferred_element_type=jnp.float32) + expand_bias
    active = jax.nn.gelu(hidden, approximate=False).astype(jnp.bfloat16)
    branches = jnp.dot(mixed, output_weight, preferred_element_type=jnp.float32)
    branches = branches + jnp.dot(active, shrink_weight, preferred_element_type=jnp.float32)
    result = (
        stream + exchange_sum(branches, "tensor") + output_bias + shrink_bias
    ).astype(jnp.bfloat16)
    upstream = cotangent.astype(jnp.float32)
    column_sum = jnp.sum(upstream, axis=0)
    width = tokens.shape[1]
    near_pick = picker(near_first, size, width)
    far_pick = picker(far_first, size, width)
    ordered = jnp.dot(
        jnp.concatenate([cotangent, lower_two, lower_one], axis=0),
        near_pick,
        preferred_element_type=jnp.float32,
    ).astype(jnp.bfloat16)
    cotangent_near, two_near, one_near = (
        ordered[:count],
        ordered[count : 2 * count],
        ordered[2 * count :],
    )
    cotangent_far = jnp.dot(cotangent, far_pick, preferred_element_type=jnp.float32).astype(
        jnp.bfloat16
    )
    shrink_sum = weight_sum(cotangent_near, active, near_first).T
    grad_active = jnp.einsum(
        "cd,fd->cf", cotangent, shrink_weight, preferred_element_type=jnp.float32
    )
    grad_hidden = grad_active * gelu_slope(hidden)
    expand_bias_grad = jnp.sum(grad_hidden, axis=0)
    lower_hidden = grad_hidden.astype(jnp.bfloat16)
    expand_sum = weight_sum(two_near, lower_hidden, near_first)
    grad_norm_two = jnp.einsum(
        "cf,df->cd", lower_hidden, expand_weight, preferred_element_type=jnp.float32
    )
    output_sum = weight_sum(cotangent_far, mixed, far_first).T
    grad_mixed = jnp.einsum(
        "cd,ed->ce", cotangent, output_weight, preferred_element_type=jnp.float32
    )
    grad_mixed = grad_mixed.astype(jnp.bfloat16).reshape(count, heads_here, HEAD_DIM)
    again = scores_of(queries, keys_rot, allowed)
    again_probs = jnp.where(allowed[None], jnp.exp(again - logsum), 0.0)
    grad_probs = jnp.einsum("ihd,jhd->hij", grad_mixed, values, preferred_element_type=jnp.float32)
    grad_values = jnp.einsum(
        "hij,ihd->jhd",
        again_probs.astype(jnp.bfloat16),
        grad_mixed,
        preferred_element_type=jnp.float32,
    )
    inner = jnp.sum(again_probs * grad_probs, axis=2, keepdims=True)
    grad_scores = (again_probs * (grad_probs - inner) * HEAD_DIM ** (-0.5)).astype(jnp.bfloat16)
    grad_queries = unrotate(
        jnp.einsum("hij,jhd->ihd", grad_scores, keys_rot, preferred_element_type=jnp.float32),
        cosine,
        sine,
    )
    grad_keys = unrotate(
        jnp.einsum("hij,ihd->jhd", grad_scores, queries, preferred_element_type=jnp.float32),
        cosine,
        sine,
    )
    grad_projected = jnp.stack(
        [
            grad_queries.reshape(count, -1),
            grad_keys.reshape(count, -1),
            grad_values.reshape(count, -1),
        ],
        axis=1,
    )
    attend_bias_grad = jnp.sum(grad_projected, axis=0)
    lower_projected = grad_projected.astype(jnp.bfloat16)
    attend_sum = weight_sum(one_near, lower_projected.reshape(count, -1), near_first)
    attend_sum = attend_sum.reshape(-1, *attend_weight.shape[1:])
    grad_norm_one = jnp.einsum(
        "ctf,dtf->cd", lower_projected, attend_weight, preferred_element_type=jnp.float32
    )
    full_one = exchange_sum(grad_norm_one, "tensor")
    full_two = exchange_sum(grad_norm_two, "tensor")
    grad_input = upstream + norm_back(full_one, scaled_one, inverse_one, first_gain)
    grad_input = grad_input + norm_back(full_two, scaled_two, inverse_two, second_gain)
    gain_one = jnp.sum(full_one * scaled_one, axis=0)
    shift_one = jnp.sum(full_one, axis=0)
    gain_two = jnp.sum(full_two * scaled_two, axis=0)
    shift_two = jnp.sum(full_two, axis=0)
    singles = [gain_one, shift_one, gain_two, shift_two, column_sum, expand_bias_grad]
    pieces = [single.reshape(size, -1) for single in singles]
    pieces.append(attend_bias_grad.reshape(3, size, -1).transpose(1, 0, 2).reshape(size, -1))
    small = jnp.concatenate(pieces, axis=1)
    order = jnp.array(block_order(near_first, size), dtype=jnp.int32)
    owner = jnp.bitwise_xor(order, lax.axis_index("dp").astype(jnp.int32))
    placed = (owner[:, None] == jnp.arange(size, dtype=jnp.int32)[None, :]).astype(jnp.float32)
    small = jnp.dot(placed, small, precision=lax.Precision.HIGHEST)
    for bit in near_first:
        half = small.shape[0] // 2
        small = small[:half] + swap(small[half:], bit)
    small = small.reshape(-1)
    ends = []
    at = 0
    for piece in pieces:
        ends.append(small[at : at + piece.shape[1]])
        at += piece.shape[1]
    (
        gain_one_sum,
        shift_one_sum,
        gain_two_sum,
        shift_two_sum,
        column_total,
        expand_bias_sum,
        attend_bias_sum,
    ) = ends
    attend_bias_sum = attend_bias_sum.reshape(3, -1)
    return (
        result,
        grad_input.astype(jnp.bfloat16),
        gain_one_sum,
        shift_one_sum,
        gain_two_sum,
        shift_two_sum,
        attend_sum,
        attend_bias_sum,
        output_sum,
        column_total,
        expand_sum,
        expand_bias_sum,
        shrink_sum,
        column_total,
    )


def solution(mesh):
    placed = (
        P("dp", None),
        P("dp", None),
        P("dp"),
        P(),
        P(),
        P(),
        P(),
        P(None, None, "tensor"),
        P(None, "tensor"),
        P("tensor", None),
        P(),
        P(None, "tensor"),
        P("tensor"),
        P("tensor", None),
        P(),
    )
    return jax.shard_map(
        local,
        mesh=mesh,
        in_specs=placed,
        out_specs=(
            P("dp", None),
            P("dp", None),
            P("dp"),
            P("dp"),
            P("dp"),
            P("dp"),
            P("dp", None, "tensor"),
            P(None, ("tensor", "dp")),
            P("tensor", "dp"),
            P("dp"),
            P("dp", "tensor"),
            P(("tensor", "dp")),
            P("tensor", "dp"),
            P("dp"),
        ),
        check_vma=False,
    )
```
